768 devices in a mesh: space: 12 (over z), member: 64 (over x, y, core).
Axes of the slice: x: 4, y: 8, z: 12, core: 2. Of those that a mesh axis runs over, the one named last changes fastest.
Arguments:
- prior_ensemble: float32 [256, 256, 1536], P('member', None, 'space'), may hold values from -12 to 12, as said below
- wind: float32 [256, 1536], P(None, 'space'), may hold values from -1 to 1
- obs_value: float32 [768, 512], P(('space', 'member')), may hold values from -6 to 6
- obs_weight: float32 [768, 512], P(('space', 'member')), may hold values from 0.25 to 4
- observed_cell_value: int32 [768, 512], P(('space', 'member')), may hold values from 0 to 511
- obs_count: int32 [768], P(('space', 'member')), may hold values from 64 to 512, as said below
Outputs:
- analysis: float32 [256, 256, 1536], P('member', None, 'space')
The draws below stay inside these ranges and needn't reach their ends.
Inputs may be any that keep to these rules, and one draw needn't show every extreme that they name: `prior_ensemble`: member states are rough from cell to cell, member scales differ. `obs_count`: some patch has all 512 slots live and some has 64 live.
All inputs are finite; a program needn't handle non-finite values.
Results may differ from the reference program's by a relative error of at most 0.0003.
Values sent between devices are 32-bit elements; how exact they have to be, the bound alone decides.
A program may use at most 32 MiB of HBM per device.

```python
import math
import jax
import jax.numpy as jnp
from jax import lax

REGION_HEIGHT = 4
TILE_WIDTH = 128
OBS_MAX = 512
SUBSTEPS = 4
NS_ITERS = 6
ENSEMBLE_SIZE = 256
NY = 256
NX = 1536
REGION_COUNT = 768
N_SPACE = 12


def draw_prior_ensemble(key, part):
    first, second = jax.random.split(jax.random.fold_in(key, 11))
    scales = jnp.exp(jax.random.uniform(first, (ENSEMBLE_SIZE, 1, 1), jnp.float32, math.log(0.3), math.log(3.0)))
    base = jnp.clip(jax.random.normal(second, (ENSEMBLE_SIZE, NY, NX), jnp.float32), -4.0, 4.0)
    return base * scales


def draw_obs_count(key, part):
    first, second, third = jax.random.split(jax.random.fold_in(key, 23), 3)
    lowest = OBS_MAX // 8
    raw = jax.random.randint(first, (REGION_COUNT,), 0, 64)
    counts = lowest + (OBS_MAX - lowest) * raw * raw // 3969
    pick = jax.random.randint(second, (), 0, REGION_COUNT)
    other = (pick + 1 + jax.random.randint(third, (), 0, REGION_COUNT - 1)) % REGION_COUNT
    counts = counts.at[pick].set(OBS_MAX)
    counts = counts.at[other].set(lowest)
    return counts.astype(jnp.int32)


def plant(values, rng, least, top_value):
    dims = values.shape
    index_at = [jax.random.randint(jax.random.fold_in(rng, axis), (), 0, dims[axis]) for axis in range(len(dims))]
    values = values.at[tuple(index_at)].set(least)
    longest = dims.index(max(dims))
    index_at[longest] = (index_at[longest] + 1) % dims[longest]
    return values.at[tuple(index_at)].set(top_value)


def levels(key, extent, pieces, low, high):
    factor_of = 1.0
    for position, parts in pieces:
        heights = jax.random.uniform(jax.random.fold_in(jax.random.fold_in(key, 6), position), (parts,), jnp.float32, low / len(pieces), high / len(pieces))
        factor_of = factor_of * jnp.repeat(jnp.exp(heights), extent[position] // parts).reshape((-1,) + (1,) * (len(extent) - 1 - position))
    return factor_of


def gaussian(own_key, shape, spread, bound, shards=(), held_as=jnp.bfloat16):
    entries = spread * jax.random.normal(own_key, shape, jnp.float32)
    if shards:
        entries = entries * levels(own_key, shape, shards, -0.22, 0.18)
    return jnp.clip(entries, -bound, bound).astype(held_as)


def setup_inputs(seed: int = 0) -> dict:
    arg_keys = jax.random.split(jax.random.key(seed), 7)
    return {
        "prior_ensemble": draw_prior_ensemble(jax.random.fold_in(arg_keys[6], 71), 0),
        "wind": jnp.clip(jax.random.uniform(arg_keys[1], (NY, NX), jnp.float32, -1.0, 1.0) * levels(arg_keys[1], (NY, NX), ((1, 12),), -0.4, 0.0), -1.0, 1.0),
        "obs_value": gaussian(arg_keys[2], (REGION_COUNT, OBS_MAX), 1.0, 6.0, ((0, 768),), jnp.float32),
        "obs_weight": jnp.clip(jnp.exp(math.log(4.0) - 2.7725887 * jax.random.uniform(arg_keys[3], (REGION_COUNT, OBS_MAX), jnp.float32) ** levels(arg_keys[3], (REGION_COUNT, OBS_MAX), ((0, 768),), -0.2, 0.2)), 0.25, 4.0),
        "observed_cell_value": plant(jax.random.randint(arg_keys[4], (REGION_COUNT, OBS_MAX), 0, REGION_HEIGHT * TILE_WIDTH), jax.random.fold_in(arg_keys[4], 1), 0, (REGION_HEIGHT * TILE_WIDTH) - 1).astype(jnp.int32),
        "obs_count": draw_obs_count(jax.random.fold_in(arg_keys[6], 71), 0),
    }


def tendency(center, east, west, wind_mid):
    pads = [(0, 0)] * (center.ndim - 2) + [(1, 1), (0, 0)]
    ypad = jnp.pad(center, pads)
    north = ypad[..., 2:, :]
    south = ypad[..., :-2, :]
    speed = wind_mid + 0.25 * jnp.tanh(center)
    return center + 0.2 * (east - 2.0 * center + west) + 0.1 * (north - 2.0 * center + south) - 0.3 * speed * (east - west)

def inverse_root(gram):
    order = gram.shape[0]
    ident = jnp.eye(order, dtype=jnp.float32)
    scale = jnp.sqrt(jnp.sum(gram * gram) + 1e-06)
    upper = gram / scale
    lower = ident
    for step in range(NS_ITERS):
        middle = 1.5 * ident - 0.5 * jnp.dot(lower, upper, precision=lax.Precision.HIGHEST)
        upper = jnp.dot(upper, middle, precision=lax.Precision.HIGHEST)
        lower = jnp.dot(middle, lower, precision=lax.Precision.HIGHEST)
    return lower / jnp.sqrt(scale)

def analyze(xb, cells, value, weight, count):
    order = xb.shape[0]
    mean = lax.optimization_barrier(jnp.sum(xb, axis=0)) / order
    pert = xb - mean
    ypert = jnp.take(pert, cells, axis=1)
    ymean = jnp.take(mean, cells)
    live = (jnp.arange(cells.shape[0], dtype=jnp.int32) < count).astype(jnp.float32)
    wts = weight * live
    gram = (order - 1.0) * jnp.eye(order, dtype=jnp.float32) + jnp.dot(ypert * wts, ypert.T, precision=lax.Precision.HIGHEST)
    rhs = jnp.dot(ypert, wts * (value - ymean), precision=lax.Precision.HIGHEST)
    root = inverse_root(gram)
    wbar = jnp.dot(root, jnp.dot(root, rhs, precision=lax.Precision.HIGHEST), precision=lax.Precision.HIGHEST)
    trans = jnp.sqrt(order - 1.0) * root + wbar[:, None]
    return mean + jnp.dot(trans.T, pert, precision=lax.Precision.HIGHEST)

def reference(prior_ensemble, wind, obs_value, obs_weight, observed_cell_value, obs_count):

    def predicted_ensemble(model_variable):
        for step in range(SUBSTEPS):
            model_variable = tendency(model_variable, jnp.roll(model_variable, -1, axis=1), jnp.roll(model_variable, 1, axis=1), wind)
        return model_variable
    predicted_vector = lax.map(predicted_ensemble, prior_ensemble)
    latitude_lines = NY // REGION_HEIGHT
    local_regions = predicted_vector.reshape(ENSEMBLE_SIZE, latitude_lines, REGION_HEIGHT, N_SPACE, TILE_WIDTH).transpose(3, 1, 0, 2, 4).reshape(REGION_COUNT, ENSEMBLE_SIZE, REGION_HEIGHT * TILE_WIDTH)
    result = lax.map(lambda items: analyze(*items), (local_regions, observed_cell_value, obs_value, obs_weight, obs_count))
    return result.reshape(N_SPACE, latitude_lines, ENSEMBLE_SIZE, REGION_HEIGHT, TILE_WIDTH).transpose(2, 1, 3, 0, 4).reshape(ENSEMBLE_SIZE, NY, NX)
```

```python
import functools
import jax
import jax.numpy as jnp
from jax import lax
from jax.experimental import pallas as pl
from jax.experimental.pallas import tpu as pltpu
from jax.sharding import PartitionSpec as P

SUBSTEPS = 4
NS_ITERS = 6
HEIGHT = 4
LANES = 128
MESH = pl.DeviceIdType.MESH
F32 = jnp.float32
BF16 = jnp.bfloat16


def halo_kernel(prior_ref, wind_ref, own_ref, left_ref, right_ref, send_sem, recv_sem):
    z = lax.axis_index("space")
    m = lax.axis_index("member")
    n = lax.axis_size("space")
    lft = lax.rem(z + n - 1, n)
    rgt = lax.rem(z + 1, n)
    barrier = pltpu.get_barrier_semaphore()
    for nb in (lft, rgt):
        pl.semaphore_signal(barrier, inc=1, device_id=(nb, m), device_id_type=MESH)
    rows = prior_ref.shape[0]
    own_ref[:, :rows] = pltpu.roll(prior_ref[...], SUBSTEPS, 1).T[:8, :]
    own_ref[:, rows:] = pltpu.roll(wind_ref[...], SUBSTEPS, 1).T[:8, :]
    pl.semaphore_wait(barrier, 2)
    to_right = pltpu.make_async_remote_copy(
        src_ref=own_ref, dst_ref=left_ref, send_sem=send_sem.at[0], recv_sem=recv_sem.at[0],
        device_id=(rgt, m), device_id_type=MESH)
    to_left = pltpu.make_async_remote_copy(
        src_ref=own_ref, dst_ref=right_ref, send_sem=send_sem.at[1], recv_sem=recv_sem.at[1],
        device_id=(lft, m), device_id_type=MESH)
    to_right.start()
    to_left.start()
    to_right.wait()
    to_left.wait()


def advance(center, east, west, ns, wind3):
    t = wind3 + 0.075 * jnp.tanh(center)
    return 0.4 * center + 0.1 * ns + 0.2 * (east + west) - t * (east - west)


def split(x):
    hi = x.astype(BF16)
    return hi, (x - hi.astype(F32)).astype(BF16)


def mul3(a, b):
    lhs = jnp.concatenate([a[0], a[0], a[1]], axis=1)
    rhs = jnp.concatenate([b[0], b[1], b[0]], axis=0)
    return jnp.dot(lhs, rhs, preferred_element_type=F32)


def main_kernel(count_ref, prior_ref, wind_ref, own_ref, left_ref, right_ref, value_ref, weight_ref,
                cells_ref, out_ref, edge, sbuf, rbuf, tbuf, obuf, pert_hi, pert_lo,
                send_sem, recv_sem):
    z = lax.axis_index("space")
    me = lax.axis_index("member")
    G = lax.axis_size("member")
    rows = prior_ref.shape[0]
    members = rows // (G * HEIGHT)
    ny = G * HEIGHT
    block = members * HEIGHT
    order = G * members
    barrier = pltpu.get_barrier_semaphore()

    def peer(o):
        return lax.rem(me + o, G)

    def greet(o, c):
        pl.semaphore_signal(barrier, inc=1, device_id=(z, peer(o)), device_id_type=MESH)
        return c

    lax.fori_loop(1, G, greet, 0)

    sub = lax.broadcasted_iota(jnp.int32, (8, rows), 0)
    row = lax.rem(lax.broadcasted_iota(jnp.int32, (8, rows), 1), ny)
    own = own_ref[...]
    low = lax.broadcasted_iota(jnp.int32, own.shape, 0) < 4
    left_all = jnp.where(low, left_ref[...], own)
    right_all = jnp.where(low, own, right_ref[...])
    strips = []
    for whole in (left_all, right_all):
        w3 = 0.3 * whole[:, rows:]
        strips.append((whole[:, :rows], jnp.concatenate([w3] * members, axis=1)))
    packed = jnp.zeros((8, rows), F32)
    for s in range(SUBSTEPS):
        (lu, lw), (ru, rw) = strips
        packed = jnp.where(sub == 2 * s + 1, pltpu.roll(lu, (2 * s + 1 - 3) % 8, 0), packed)
        packed = jnp.where(sub == 2 * s, pltpu.roll(ru, (2 * s - 4) % 8, 0), packed)
        if s < SUBSTEPS - 1:
            new = []
            for u, w in strips:
                north = jnp.where(row == ny - 1, 0.0, pltpu.roll(u, rows - 1, 1))
                south = jnp.where(row == 0, 0.0, pltpu.roll(u, 1, 1))
                new.append((advance(u, pltpu.roll(u, 7, 0), pltpu.roll(u, 1, 0), north + south, w), w))
            strips = new
    edge[:, :8] = packed.T

    lane = lax.broadcasted_iota(jnp.int32, (G, LANES), 1)
    patch = lax.broadcasted_iota(jnp.int32, (G, LANES), 0)
    wind3 = [0.3 * wind_ref[pl.ds(j, G, stride=HEIGHT), :] for j in range(HEIGHT)]

    def forecast(ml, carry):
        base = ml * ny
        c = [prior_ref[pl.ds(base + j, G, stride=HEIGHT), :] for j in range(HEIGHT)]
        h = [edge[pl.ds(base + j, G, stride=HEIGHT), :] for j in range(HEIGHT)]
        for s in range(SUBSTEPS):
            new = []
            for j in range(HEIGHT):
                hs = pltpu.roll(h[j], LANES - (2 * s + 1), 1)
                west = jnp.where(lane == 0, hs, pltpu.roll(c[j], 1, 1))
                east = jnp.where(lane == LANES - 1, hs, pltpu.roll(c[j], LANES - 1, 1))
                north = c[j + 1] if j < HEIGHT - 1 else jnp.where(
                    patch == G - 1, 0.0, pltpu.roll(c[0], G - 1, 0))
                south = c[j - 1] if j else jnp.where(patch == 0, 0.0, pltpu.roll(c[HEIGHT - 1], 1, 0))
                new.append(advance(c[j], east, west, north + south, wind3[j]))
            c = new
        for j in range(HEIGHT):
            sbuf[pl.ds(ml * HEIGHT + j, G, stride=block), :] = c[j]
        return carry

    lax.fori_loop(0, members, forecast, 0)
    pl.semaphore_wait(barrier, G - 1)

    def exchange(src, dst, k):
        def copy(o):
            to = peer(o)
            return pltpu.make_async_remote_copy(
                src_ref=src.at[pl.ds(pl.multiple_of(to * block, block), block), :],
                dst_ref=dst.at[pl.ds(pl.multiple_of(me * block, block), block), :],
                send_sem=send_sem.at[k], recv_sem=recv_sem.at[k],
                device_id=(z, to), device_id_type=MESH)

        def start(o, c):
            copy(o).start()
            return c

        lax.fori_loop(1, G, start, 0)
        mine = pl.ds(pl.multiple_of(me * block, block), block)
        dst[mine, :] = src[mine, :]

    def settle(src, k, sem):
        many = src.at[pl.ds(0, (G - 1) * block), :]
        pltpu.make_async_copy(many, many, sem.at[k]).wait()

    exchange(sbuf, rbuf, 0)

    slots = cells_ref.shape[1]
    live = lax.broadcasted_iota(jnp.int32, (1, slots), 1) < count_ref[0]
    wts = jnp.where(live, weight_ref[...], 0.0)
    wval = wts * value_ref[...]
    dsum = [jnp.zeros((8, LANES), F32) for _ in range(HEIGHT)]
    esum = [jnp.zeros((8, LANES), F32) for _ in range(HEIGHT)]
    cell_of = lax.broadcasted_iota(jnp.int32, (LANES, LANES), 1)
    for k in range(slots // LANES):
        part = slice(k * LANES, (k + 1) * LANES)
        cs = jnp.broadcast_to(cells_ref[:, part], (LANES, LANES)).T
        ws = jnp.broadcast_to(wts[:, part], (LANES, LANES)).T
        vs = jnp.broadcast_to(wval[:, part], (LANES, LANES)).T
        for j in range(HEIGHT):
            hit = cs == cell_of + j * LANES
            dsum[j] += jnp.sum(jnp.where(hit, ws, 0.0).reshape(LANES // 8, 8, LANES), axis=0)
            esum[j] += jnp.sum(jnp.where(hit, vs, 0.0).reshape(LANES // 8, 8, LANES), axis=0)
    dcell = [jnp.sum(x, axis=0, keepdims=True) for x in dsum]
    ecell = [jnp.sum(x, axis=0, keepdims=True) for x in esum]

    settle(rbuf, 0, recv_sem)

    mean = []
    rcell = []
    scaled = []
    for j in range(HEIGHT):
        x = jnp.concatenate(
            [rbuf[pl.ds(ml * HEIGHT + j, G, stride=block), :] for ml in range(members)], axis=0)
        mu = jnp.sum(x, axis=0, keepdims=True) * (1.0 / order)
        p = x - mu
        hi, lo = split(p)
        cols = slice(j * LANES, (j + 1) * LANES)
        pert_hi[:, cols] = hi
        pert_lo[:, cols] = lo
        scaled.append(split(p * dcell[j]))
        mean.append(mu)
        rcell.append(ecell[j] - dcell[j] * mu)
    a_hi = jnp.concatenate([s[0] for s in scaled], axis=1)
    a_lo = jnp.concatenate([s[1] for s in scaled], axis=1)
    nt = (((1,), (1,)), ((), ()))
    eye = (lax.broadcasted_iota(jnp.int32, (order, order), 0)
           == lax.broadcasted_iota(jnp.int32, (order, order), 1))
    gram = lax.dot_general(
        jnp.concatenate([a_hi, a_hi, a_lo], axis=1),
        jnp.concatenate([pert_hi[...], pert_lo[...], pert_hi[...]], axis=1),
        nt, preferred_element_type=F32)
    gram = gram + jnp.where(eye, order - 1.0, 0.0)
    total = jnp.sum(jnp.sum(gram * gram, axis=0, keepdims=True), axis=1, keepdims=True) + 1e-06
    scale = jnp.sqrt(total)
    y = gram / scale
    diag = jnp.where(eye, 1.5, 0.0)
    mid = diag - 0.5 * y
    ms = split(mid)
    y = mul3(split(y), ms)
    zmat = mid
    for step in range(1, NS_ITERS):
        ys, zs = split(y), split(zmat)
        ms = split(diag - 0.5 * mul3(zs, ys))
        if step < NS_ITERS - 1:
            y = mul3(ys, ms)
        zmat = mul3(zs, ms)
    root = zmat / jnp.sqrt(scale)
    dev = mul3(split(root), (pert_hi[...], pert_lo[...]))
    u = jnp.zeros((order, 1), F32)
    for j in range(HEIGHT):
        u = u + jnp.sum(dev[:, j * LANES:(j + 1) * LANES] * rcell[j], axis=1, keepdims=True)
    for j in range(HEIGHT):
        dj = dev[:, j * LANES:(j + 1) * LANES]
        shift = mean[j] + jnp.sum(dj * u, axis=0, keepdims=True)
        res = shift + jnp.sqrt(jnp.full((1, 1), order - 1.0, F32)) * dj
        for ml in range(members):
            tbuf[pl.ds(ml * HEIGHT + j, G, stride=block), :] = res[ml * G:(ml + 1) * G, :]

    exchange(tbuf, obuf, 1)
    settle(rbuf, 0, send_sem)
    settle(obuf, 1, recv_sem)
    for ml in range(members):
        for j in range(HEIGHT):
            out_ref[pl.ds(ml * ny + j, G, stride=HEIGHT), :] = obuf[
                pl.ds(ml * HEIGHT + j, G, stride=block), :]
    settle(obuf, 1, send_sem)


def local(prior_ensemble, wind, obs_value, obs_weight, observed_cell_value, obs_count):
    members, ny, columns = prior_ensemble.shape
    rows = members * ny
    order = members * lax.axis_size("member")
    prior = prior_ensemble.reshape(rows, columns)
    vmem = pl.BlockSpec(memory_space=pltpu.VMEM)
    strip = jax.ShapeDtypeStruct((8, rows + ny), F32)
    own, left, right = pl.pallas_call(
        halo_kernel,
        out_shape=(strip, strip, strip),
        in_specs=[vmem] * 2,
        out_specs=(vmem,) * 3,
        scratch_shapes=[pltpu.SemaphoreType.DMA((2,)), pltpu.SemaphoreType.DMA((2,))],
        compiler_params=pltpu.CompilerParams(collective_id=0, has_side_effects=True),
        name="halo",
    )(prior, wind)
    big = pltpu.VMEM((rows, LANES), F32)
    half = pltpu.VMEM((order, HEIGHT * LANES), BF16)
    out = pl.pallas_call(
        main_kernel,
        out_shape=jax.ShapeDtypeStruct((rows, columns), F32),
        in_specs=[pl.BlockSpec(memory_space=pltpu.SMEM)] + [vmem] * 8,
        out_specs=vmem,
        scratch_shapes=[big] * 5 + [half] * 2
        + [pltpu.SemaphoreType.DMA((2,)), pltpu.SemaphoreType.DMA((2,))],
        compiler_params=pltpu.CompilerParams(
            collective_id=1, has_side_effects=True, vmem_limit_bytes=40 * 1024 * 1024),
        name="forecast_analysis",
    )(obs_count, prior, wind, own, left, right, obs_value, obs_weight, observed_cell_value)
    return out.reshape(members, ny, columns)


def solution(mesh):
    in_specs = (
        P("member", None, "space"),
        P(None, "space"),
        P(("space", "member"), None),
        P(("space", "member"), None),
        P(("space", "member"), None),
        P(("space", "member")),
    )
    out_specs = P("member", None, "space")
    return jax.shard_map(local, mesh=mesh, in_specs=in_specs, out_specs=out_specs, check_vma=False)
```

```python
import functools
import jax
import jax.numpy as jnp
from jax import lax
from jax.experimental import pallas as pl
from jax.experimental.pallas import tpu as pltpu
from jax.sharding import PartitionSpec as P

SUBSTEPS = 4
NS_ITERS = 6
HEIGHT = 4
LANES = 128
VMEM_BYTES = 16 * 1024 * 1024
MESH = pl.DeviceIdType.MESH
F32 = jnp.float32
BF16 = jnp.bfloat16


def advance(center, east, west, ns, wind3):
    t = wind3 + 0.075 * jnp.tanh(center)
    return 0.4 * center + 0.1 * ns + 0.2 * (east + west) - t * (east - west)


def split(x):
    hi = x.astype(BF16)
    return hi, (x - hi.astype(F32)).astype(BF16)


def mul3(a, b):
    lhs = jnp.concatenate([a[0], a[0], a[1]], axis=1)
    rhs = jnp.concatenate([b[0], b[1], b[0]], axis=0)
    return jnp.dot(lhs, rhs, preferred_element_type=F32)


def main_kernel(count_hbm, prior_hbm, wind_hbm, value_hbm, weight_hbm, cells_hbm, obuf,
                count_ref, prior_ref, wind_ref, value_ref, weight_ref, cells_ref,
                own_ref, left_ref, right_ref, edge, sbuf, rbuf, tbuf, esend, erecv, pert_hi, pert_lo,
                in_sem, halo_send, halo_recv, send_sem, recv_sem, plane_sem, space_sem):
    z = lax.axis_index("space")
    me = lax.axis_index("member")
    Z = lax.axis_size("space")
    G = lax.axis_size("member")
    rows = prior_ref.shape[0]
    members = rows // (G * HEIGHT)
    ny = G * HEIGHT
    block = members * HEIGHT
    order = G * members
    lft = lax.rem(z + Z - 1, Z)
    rgt = lax.rem(z + 1, Z)
    core = lax.rem(me, 2)
    chip = me // 2
    loads = [pltpu.make_async_copy(src, dst, in_sem.at[i]) for i, (src, dst) in enumerate((
        (prior_hbm, prior_ref), (wind_hbm, wind_ref), (cells_hbm, cells_ref),
        (weight_hbm, weight_ref), (value_hbm, value_ref), (count_hbm, count_ref)))]
    for load in loads:
        load.start()
    barrier = pltpu.get_barrier_semaphore()

    def greet(o, c):
        to = lax.rem(chip + o, G // 2) * 2
        pl.semaphore_signal(barrier, inc=1, device_id=(z, to), device_id_type=MESH)
        return c

    lax.fori_loop(1, G // 2, greet, 0)

    @pl.when(core == 1)
    def _():
        pl.semaphore_signal(barrier, inc=1, device_id=(z, me - 1), device_id_type=MESH)

    for nb in (lft, rgt):
        pl.semaphore_signal(barrier, inc=1, device_id=(nb, chip * 2 + 1), device_id_type=MESH)

    patch = lax.broadcasted_iota(jnp.int32, (G, LANES), 0)
    loads[0].wait()
    loads[1].wait()
    wind3 = [0.3 * wind_ref[pl.ds(j, G, stride=HEIGHT), :] for j in range(HEIGHT)]

    def forecast(ml, carry):
        base = ml * ny
        c = [prior_ref[pl.ds(base + j, G, stride=HEIGHT), :] for j in range(HEIGHT)]
        for s in range(SUBSTEPS):
            new = []
            for j in range(HEIGHT):
                west = pltpu.roll(c[j], 1, 1)
                east = pltpu.roll(c[j], LANES - 1, 1)
                north = c[j + 1] if j < HEIGHT - 1 else jnp.where(
                    patch == G - 1, 0.0, pltpu.roll(c[0], G - 1, 0))
                south = c[j - 1] if j else jnp.where(patch == 0, 0.0, pltpu.roll(c[HEIGHT - 1], 1, 0))
                new.append(advance(c[j], east, west, north + south, wind3[j]))
            c = new
        for j in range(HEIGHT):
            sbuf[pl.ds(ml * HEIGHT + j, G, stride=block), :] = c[j]
        return carry

    lax.fori_loop(0, members, forecast, 0)

    @pl.when(core == 0)
    def _():
        pl.semaphore_wait(barrier, G - 1)
        pl.semaphore_signal(plane_sem, inc=1, device_id=(z, chip * 2 + 1), device_id_type=MESH)

    @pl.when(core == 1)
    def _():
        pl.semaphore_wait(plane_sem, 1)

    def exchange(make):
        ring = 8 if G >= 16 else G // 2
        columns = G // 2 // ring

        def both(k, c):
            t = lax.rem(k, ring)
            u = k // ring
            dy = ring // 2 + (1 - 2 * lax.rem(t, 2)) * ((t + 1) // 2)
            dx = columns // 2 + (1 - 2 * lax.rem(u, 2)) * ((u + 1) // 2)
            y = lax.rem(lax.rem(chip, ring) + dy, ring)
            x = lax.rem(chip // ring + dx, columns)
            to = (x * ring + y) * 2
            make(to + core).start()
            make(to + 1 - core).start()
            return c

        lax.fori_loop(0, G // 2 - 1, both, 0)
        make(chip * 2 + 1 - core).start()

    def blocks(src, dst, k):
        def make(to):
            return pltpu.make_async_remote_copy(
                src_ref=src.at[pl.ds(pl.multiple_of(to * block, block), block), :],
                dst_ref=dst.at[pl.ds(pl.multiple_of(me * block, block), block), :],
                send_sem=send_sem.at[k], recv_sem=recv_sem.at[k],
                device_id=(z, to), device_id_type=MESH)

        exchange(make)
        mine = pl.ds(pl.multiple_of(me * block, block), block)
        dst[mine, :] = src[mine, :]

    def settle(src, k, sem):
        many = src.at[pl.ds(0, (G - 1) * block), :]
        pltpu.make_async_copy(many, many, sem.at[k]).wait()

    blocks(sbuf, rbuf, 0)

    for ref, at in ((prior_ref, slice(0, rows)), (wind_ref, slice(rows, rows + ny))):
        turned = pltpu.roll(ref[...], SUBSTEPS, 1).T
        own_ref[0:8, at] = turned[0:8, :]
        own_ref[8:16, at] = turned[8:16, :]
        own_ref[16:24, at] = turned[LANES - 8:LANES, :]

    @pl.when(core == 1)
    def _():
        pl.semaphore_wait(barrier, 4)
        pl.semaphore_signal(space_sem, inc=1, device_id=(z, chip * 2), device_id_type=MESH)

    @pl.when(core == 0)
    def _():
        pl.semaphore_wait(space_sem, 1)

    halos = [pltpu.make_async_remote_copy(
        src_ref=own_ref.at[0:8, :], dst_ref=dst, send_sem=halo_send.at[k], recv_sem=halo_recv.at[k],
        device_id=(nb, me), device_id_type=MESH)
        for k, (dst, nb) in enumerate(((left_ref, rgt), (right_ref, lft)))]
    for halo in halos:
        halo.start()

    for load in loads[2:]:
        load.wait()
    slots = cells_ref.shape[1]
    live = lax.broadcasted_iota(jnp.int32, (1, slots), 1) < count_ref[0]
    wts = jnp.where(live, weight_ref[...], 0.0)
    wval = wts * value_ref[...]
    dsum = [jnp.zeros((8, LANES), F32) for _ in range(HEIGHT)]
    esum = [jnp.zeros((8, LANES), F32) for _ in range(HEIGHT)]
    cell_of = lax.broadcasted_iota(jnp.int32, (LANES, LANES), 1)
    for k in range(slots // LANES):
        part = slice(k * LANES, (k + 1) * LANES)
        cs = jnp.broadcast_to(cells_ref[:, part], (LANES, LANES)).T
        ws = jnp.broadcast_to(wts[:, part], (LANES, LANES)).T
        vs = jnp.broadcast_to(wval[:, part], (LANES, LANES)).T
        for j in range(HEIGHT):
            hit = cs == cell_of + j * LANES
            dsum[j] += jnp.sum(jnp.where(hit, ws, 0.0).reshape(LANES // 8, 8, LANES), axis=0)
            esum[j] += jnp.sum(jnp.where(hit, vs, 0.0).reshape(LANES // 8, 8, LANES), axis=0)
    dcell = [jnp.sum(x, axis=0, keepdims=True) for x in dsum]
    ecell = [jnp.sum(x, axis=0, keepdims=True) for x in esum]

    for halo in halos:
        halo.wait()
    low = lax.broadcasted_iota(jnp.int32, (8, rows + ny), 0) < 4
    first = own_ref[0:8, :]
    left_all = jnp.concatenate([jnp.where(low, left_ref[...], first), own_ref[8:16, :]], axis=0)
    right_all = jnp.concatenate([own_ref[16:24, :], jnp.where(low, first, right_ref[...])], axis=0)
    row = lax.rem(lax.broadcasted_iota(jnp.int32, (16, rows), 1), ny)
    ends = []
    for whole in (left_all, right_all):
        w3 = 0.3 * whole[:, rows:]
        w = jnp.concatenate([w3] * members, axis=1)
        x = whole[:, :rows]
        for s in range(SUBSTEPS):
            north = jnp.where(row == ny - 1, 0.0, pltpu.roll(x, rows - 1, 1))
            south = jnp.where(row == 0, 0.0, pltpu.roll(x, 1, 1))
            x = advance(x, pltpu.roll(x, 15, 0), pltpu.roll(x, 1, 0), north + south, w)
        ends.append(x)
    edge[:, :8] = jnp.where(low[:, :rows], ends[1][8:16, :], ends[0][0:8, :]).T
    lane = lax.broadcasted_iota(jnp.int32, (G, LANES), 1)
    packed = jnp.zeros((G, LANES), F32)
    for q in range(block):
        ml, j = q // HEIGHT, q % HEIGHT
        part = edge[pl.ds(ml * ny + j, G, stride=HEIGHT), :]
        packed = jnp.where(lane // 8 == q, pltpu.roll(part, 8 * q, 1), packed)
    esend[...] = packed.reshape(G, 1, LANES)

    def make_edge(to):
        return pltpu.make_async_remote_copy(
            src_ref=esend.at[pl.ds(to, 1)], dst_ref=erecv.at[pl.ds(me, 1)],
            send_sem=send_sem.at[2], recv_sem=recv_sem.at[2],
            device_id=(z, to), device_id_type=MESH)

    exchange(make_edge)
    erecv[pl.ds(me, 1)] = esend[pl.ds(me, 1)]
    settle(rbuf, 0, recv_sem)
    edges = erecv.at[pl.ds(0, G - 1)]
    pltpu.make_async_copy(edges, edges, recv_sem.at[2]).wait()
    got = erecv[...].reshape(G, LANES)
    outer = (lane < 4) | (lane >= LANES - 4)

    mean = []
    rcell = []
    scaled = []
    for j in range(HEIGHT):
        x = jnp.concatenate(
            [jnp.where(outer, pltpu.roll(got, (LANES - 4 - 8 * (ml * HEIGHT + j)) % LANES, 1),
                       rbuf[pl.ds(ml * HEIGHT + j, G, stride=block), :]) for ml in range(members)],
            axis=0)
        mu = jnp.sum(x, axis=0, keepdims=True) * (1.0 / order)
        p = x - mu
        hi, lo = split(p)
        cols = slice(j * LANES, (j + 1) * LANES)
        pert_hi[:, cols] = hi
        pert_lo[:, cols] = lo
        scaled.append(split(p * dcell[j]))
        mean.append(mu)
        rcell.append(ecell[j] - dcell[j] * mu)
    a_hi = jnp.concatenate([s[0] for s in scaled], axis=1)
    a_lo = jnp.concatenate([s[1] for s in scaled], axis=1)
    nt = (((1,), (1,)), ((), ()))
    eye = (lax.broadcasted_iota(jnp.int32, (order, order), 0)
           == lax.broadcasted_iota(jnp.int32, (order, order), 1))
    gram = lax.dot_general(
        jnp.concatenate([a_hi, a_hi, a_lo], axis=1),
        jnp.concatenate([pert_hi[...], pert_lo[...], pert_hi[...]], axis=1),
        nt, preferred_element_type=F32)
    gram = gram + jnp.where(eye, order - 1.0, 0.0)
    total = jnp.sum(jnp.sum(gram * gram, axis=0, keepdims=True), axis=1, keepdims=True) + 1e-06
    scale = jnp.sqrt(total)
    y = gram / scale
    diag = jnp.where(eye, 1.5, 0.0)
    mid = diag - 0.5 * y
    ms = split(mid)
    y = mul3(split(y), ms)
    zmat = mid
    for step in range(1, NS_ITERS):
        ys, zs = split(y), split(zmat)
        ms = split(diag - 0.5 * mul3(zs, ys))
        if step < NS_ITERS - 1:
            y = mul3(ys, ms)
        zmat = mul3(zs, ms)
    root = zmat / jnp.sqrt(scale)
    dev = mul3(split(root), (pert_hi[...], pert_lo[...]))
    u = jnp.zeros((order, 1), F32)
    for j in range(HEIGHT):
        u = u + jnp.sum(dev[:, j * LANES:(j + 1) * LANES] * rcell[j], axis=1, keepdims=True)
    for j in range(HEIGHT):
        dj = dev[:, j * LANES:(j + 1) * LANES]
        shift = mean[j] + jnp.sum(dj * u, axis=0, keepdims=True)
        res = shift + jnp.sqrt(jnp.full((1, 1), order - 1.0, F32)) * dj
        for ml in range(members):
            tbuf[pl.ds(ml * HEIGHT + j, G, stride=block), :] = res[ml * G:(ml + 1) * G, :]

    blocks(tbuf, obuf, 1)
    settle(sbuf, 0, send_sem)
    pltpu.make_async_copy(edges, edges, send_sem.at[2]).wait()
    settle(obuf, 1, recv_sem)
    settle(obuf, 1, send_sem)


def place_kernel(blocks_ref, out_hbm, tile, sem):
    rows = blocks_ref.shape[0]
    G = lax.axis_size("member")
    ny = G * HEIGHT
    members = rows // ny
    copies = []
    for ml in range(members):
        for j in range(HEIGHT):
            tile[pl.ds(ml * ny + j, G, stride=HEIGHT), :] = blocks_ref[
                pl.ds(ml * HEIGHT + j, G, stride=members * HEIGHT), :]
        span = pl.ds(ml * ny, ny)
        copies.append(pltpu.make_async_copy(tile.at[span, :], out_hbm.at[span, :], sem.at[ml]))
        copies[-1].start()
    for copy in copies:
        copy.wait()


def local(prior_ensemble, wind, obs_value, obs_weight, observed_cell_value, obs_count):
    members, ny, columns = prior_ensemble.shape
    rows = members * ny
    order = members * lax.axis_size("member")
    prior = prior_ensemble.reshape(rows, columns)
    vmem = pl.BlockSpec(memory_space=pltpu.VMEM)
    hbm = pl.BlockSpec(memory_space=pltpu.HBM)
    slots = obs_value.shape[1]
    big = pltpu.VMEM((rows, LANES), F32)
    strip = pltpu.VMEM((8, rows + ny), F32)
    half = pltpu.VMEM((order, HEIGHT * LANES), BF16)
    dma = pltpu.SemaphoreType.DMA
    blocks = pl.pallas_call(
        main_kernel,
        out_shape=pltpu.VMEM((rows, columns), F32),
        in_specs=[hbm] * 6,
        out_specs=vmem,
        scratch_shapes=[
            pltpu.SMEM((1,), jnp.int32), big, pltpu.VMEM((ny, LANES), F32),
            pltpu.VMEM((1, slots), F32), pltpu.VMEM((1, slots), F32),
            pltpu.VMEM((1, slots), jnp.int32)]
        + [pltpu.VMEM((24, rows + ny), F32)] + [strip] * 2 + [big] * 4
        + [pltpu.VMEM((order // members, 1, LANES), F32)] * 2 + [half] * 2
        + [dma((6,)), dma((2,)), dma((2,)), dma((3,)), dma((3,))]
        + [pltpu.SemaphoreType.REGULAR] * 2,
        compiler_params=pltpu.CompilerParams(
            collective_id=0, has_side_effects=True, vmem_limit_bytes=VMEM_BYTES),
        name="forecast_analysis",
    )(obs_count, *(pltpu.with_memory_space_constraint(a, pltpu.HBM) for a in (
        prior, wind, obs_value, obs_weight, observed_cell_value)))
    out = pl.pallas_call(
        place_kernel,
        out_shape=jax.ShapeDtypeStruct((rows, columns), F32),
        in_specs=[vmem],
        out_specs=hbm,
        scratch_shapes=[big, dma((members,))],
        compiler_params=pltpu.CompilerParams(vmem_limit_bytes=4 * 1024 * 1024),
        name="place",
    )(pltpu.with_memory_space_constraint(blocks, pltpu.VMEM))
    return out.reshape(members, ny, columns)


def solution(mesh):
    in_specs = (
        P("member", None, "space"),
        P(None, "space"),
        P(("space", "member"), None),
        P(("space", "member"), None),
        P(("space", "member"), None),
        P(("space", "member")),
    )
    out_specs = P("member", None, "space")
    return jax.shard_map(local, mesh=mesh, in_specs=in_specs, out_specs=out_specs, check_vma=False)
```

```python
import functools
import jax
import jax.numpy as jnp
from jax import lax
from jax.experimental import pallas as pl
from jax.experimental.pallas import tpu as pltpu
from jax.sharding import PartitionSpec as P

SUBSTEPS = 4
NS_ITERS = 6
HEIGHT = 4
LANES = 128
VMEM_BYTES = 16 * 1024 * 1024
MESH = pl.DeviceIdType.MESH
F32 = jnp.float32
BF16 = jnp.bfloat16


def advance(center, east, west, ns, wind3):
    t = wind3 + 0.075 * jnp.tanh(center)
    return 0.4 * center + 0.1 * ns + 0.2 * (east + west) - t * (east - west)


def turns(n):
    return [n // 2 + (1 - 2 * (t % 2)) * ((t + 1) // 2) for t in range(n)]


def split(x):
    hi = x.astype(BF16)
    return hi, (x - hi.astype(F32)).astype(BF16)


def mul3(a, b):
    lhs = jnp.concatenate([a[0], a[0], a[1]], axis=1)
    rhs = jnp.concatenate([b[0], b[1], b[0]], axis=0)
    return jnp.dot(lhs, rhs, preferred_element_type=F32)


def main_kernel(count_hbm, prior_hbm, wind_hbm, value_hbm, weight_hbm, cells_hbm, obuf,
                count_ref, prior_ref, wind_ref, value_ref, weight_ref, cells_ref,
                own_ref, left_ref, right_ref, edge, sbuf, lbuf, rbuf, tbuf, esend, erecv, pert_hi, pert_lo,
                in_sem, halo_send, halo_recv, send_sem, recv_sem, plane_sem, space_sem, first_sem):
    z = lax.axis_index("space")
    me = lax.axis_index("member")
    Z = lax.axis_size("space")
    G = lax.axis_size("member")
    rows = prior_ref.shape[0]
    members = rows // (G * HEIGHT)
    ny = G * HEIGHT
    block = members * HEIGHT
    order = G * members
    lft = lax.rem(z + Z - 1, Z)
    rgt = lax.rem(z + 1, Z)
    core = lax.rem(me, 2)
    chip = me // 2
    loads = [pltpu.make_async_copy(src, dst, in_sem.at[i]) for i, (src, dst) in enumerate((
        (prior_hbm, prior_ref), (wind_hbm, wind_ref), (cells_hbm, cells_ref),
        (weight_hbm, weight_ref), (value_hbm, value_ref), (count_hbm, count_ref)))]
    for load in loads:
        load.start()
    barrier = pltpu.get_barrier_semaphore()
    first_in, herald, relay = 0, 2, 4

    @pl.when(me != first_in)
    def _():
        def greet(c, carry):
            @pl.when(c * 2 != me)
            def _():
                pl.semaphore_signal(barrier, inc=1, device_id=(z, c * 2), device_id_type=MESH)
            return carry

        lax.fori_loop(relay // 2, G // 2, greet, 0)

    @pl.when(me == first_in)
    def _():
        pl.semaphore_signal(barrier, inc=1, device_id=(z, herald), device_id_type=MESH)

    @pl.when(core == 0)
    def _():
        pl.semaphore_signal(barrier, inc=1, device_id=(z, me + 1), device_id_type=MESH)

    for nb in (lft, rgt):
        pl.semaphore_signal(barrier, inc=1, device_id=(nb, chip * 2 + 1), device_id_type=MESH)

    patch = lax.broadcasted_iota(jnp.int32, (G, LANES), 0)
    loads[0].wait()
    loads[1].wait()
    wind3 = [0.3 * wind_ref[pl.ds(j, G, stride=HEIGHT), :] for j in range(HEIGHT)]

    def forecast(ml, carry):
        base = ml * ny
        c = [prior_ref[pl.ds(base + j, G, stride=HEIGHT), :] for j in range(HEIGHT)]
        for s in range(SUBSTEPS):
            new = []
            for j in range(HEIGHT):
                west = pltpu.roll(c[j], 1, 1)
                east = pltpu.roll(c[j], LANES - 1, 1)
                north = c[j + 1] if j < HEIGHT - 1 else jnp.where(
                    patch == G - 1, 0.0, pltpu.roll(c[0], G - 1, 0))
                south = c[j - 1] if j else jnp.where(patch == 0, 0.0, pltpu.roll(c[HEIGHT - 1], 1, 0))
                new.append(advance(c[j], east, west, north + south, wind3[j]))
            c = new
        for j in range(HEIGHT):
            sbuf[pl.ds(ml * HEIGHT + j, G, stride=block), :] = c[j]
        return carry

    ring = 8 if G >= 16 else G // 2
    columns = G // 2 // ring
    row_of = lax.rem(chip, ring)
    column_of = chip // ring
    near = [lax.rem(row_of + dy, ring) * 2 for dy in turns(ring)]
    cores = (core, 1 - core)

    across = turns(columns)
    early = columns - 1

    def exchange(make, first=0, last=columns, all_members=False):
        def send(to):
            if all_members:
                make(to)
            else:
                pl.when(to != first_in)(lambda: make(to))

        def column(u, c):
            dx = columns // 2 + (1 - 2 * lax.rem(u, 2)) * ((u + 1) // 2)
            there = lax.rem(column_of + dx, columns) * (ring * 2)
            for y2 in near:
                for c2 in cores:
                    send(there + y2 + c2)
            return c

        lax.fori_loop(first, min(last, columns - 1), column, 0)
        if last == columns:
            here = column_of * (ring * 2)
            for y2 in near[:-1]:
                for c2 in cores:
                    send(here + y2 + c2)
            send(here + near[-1] + cores[1])

    def block_copy(src, dst, k):
        def make(to):
            pltpu.make_async_remote_copy(
                src_ref=src.at[pl.ds(pl.multiple_of(to * block, block), block), :],
                dst_ref=dst.at[pl.ds(pl.multiple_of(me * block, block), block), :],
                send_sem=send_sem.at[k], recv_sem=recv_sem.at[k],
                device_id=(z, to), device_id_type=MESH).start()

        return make

    def keep(src, dst):
        mine = pl.ds(pl.multiple_of(me * block, block), block)
        dst[mine, :] = src[mine, :]

    def settle(src, k, sem):
        many = src.at[pl.ds(0, (G - 1) * block), :]
        pltpu.make_async_copy(many, many, sem.at[k]).wait()


    def tell(sem, to):
        pl.semaphore_signal(sem, inc=1, device_id=(z, to), device_id_type=MESH)

    for ref, at in ((prior_ref, slice(0, rows)), (wind_ref, slice(rows, rows + ny))):
        turned = pltpu.roll(ref[...], SUBSTEPS, 1).T
        own_ref[0:8, at] = turned[0:8, :]
        own_ref[8:16, at] = turned[8:16, :]
        own_ref[16:24, at] = turned[LANES - 8:LANES, :]

    halos = [pltpu.make_async_remote_copy(
        src_ref=own_ref.at[0:8, :], dst_ref=dst, send_sem=halo_send.at[k], recv_sem=halo_recv.at[k],
        device_id=(nb, me), device_id_type=MESH)
        for k, (dst, nb) in enumerate(((left_ref, rgt), (right_ref, lft)))]

    def send_halos():
        @pl.when(core == 1)
        def _():
            pl.semaphore_wait(barrier, 5)
            tell(space_sem, me - 1)

        @pl.when(core == 0)
        def _():
            pl.semaphore_wait(space_sem, 1)

        for halo in halos:
            halo.start()

    @pl.when(z != 0)
    def _():
        send_halos()

    lax.fori_loop(0, members, forecast, 0)

    @pl.when((core == 0) & (me >= relay))
    def _():
        pl.semaphore_wait(barrier, G - 2)
        tell(plane_sem, me + 1)

        @pl.when(me == relay)
        def _():
            for to in range(1, relay):
                tell(plane_sem, to)

    @pl.when((core == 1) | (me == herald))
    def _():
        pl.semaphore_wait(plane_sem, 1)

    @pl.when(me == herald)
    def _():
        pl.semaphore_wait(barrier, 1)

        def pass_on(o, carry):
            tell(first_sem, lax.rem(me + o, G))
            return carry

        lax.fori_loop(1, G, pass_on, 0)

    @pl.when(me == first_in)
    def _():
        pl.semaphore_wait(first_sem, 1)

    exchange(block_copy(sbuf, rbuf, 0), 0, early)

    @pl.when(z == 0)
    def _():
        send_halos()


    for halo in halos:
        halo.wait()
    low = lax.broadcasted_iota(jnp.int32, (8, rows + ny), 0) < 4
    first = own_ref[0:8, :]
    left_all = jnp.concatenate([jnp.where(low, left_ref[...], first), own_ref[8:16, :]], axis=0)
    right_all = jnp.concatenate([own_ref[16:24, :], jnp.where(low, first, right_ref[...])], axis=0)
    row = lax.rem(lax.broadcasted_iota(jnp.int32, (16, rows), 1), ny)
    ends = []
    for whole in (left_all, right_all):
        w3 = 0.3 * whole[:, rows:]
        w = jnp.concatenate([w3] * members, axis=1)
        x = whole[:, :rows]
        for s in range(SUBSTEPS):
            north = jnp.where(row == ny - 1, 0.0, pltpu.roll(x, rows - 1, 1))
            south = jnp.where(row == 0, 0.0, pltpu.roll(x, 1, 1))
            x = advance(x, pltpu.roll(x, 15, 0), pltpu.roll(x, 1, 0), north + south, w)
        ends.append(x)
    edge[:, :8] = jnp.where(low[:, :rows], ends[1][8:16, :], ends[0][0:8, :]).T
    lane = lax.broadcasted_iota(jnp.int32, (G, LANES), 1)
    outer = (lane < 4) | (lane >= LANES - 4)
    parts = [edge[pl.ds(q // HEIGHT * ny + q % HEIGHT, G, stride=HEIGHT), :] for q in range(block)]
    packed = jnp.zeros((G, LANES), F32)
    for q in range(block):
        packed = jnp.where(lane // 8 == q, pltpu.roll(parts[q], 8 * q, 1), packed)
    esend[...] = packed.reshape(G, 1, LANES)

    def make_edge(to):
        pltpu.make_async_remote_copy(
            src_ref=esend.at[pl.ds(to, 1)], dst_ref=erecv.at[pl.ds(me, 1)],
            send_sem=send_sem.at[2], recv_sem=recv_sem.at[2],
            device_id=(z, to), device_id_type=MESH).start()

    exchange(make_edge, 0, early)
    for q in range(block):
        mine = pl.ds(q, G, stride=block)
        lbuf[mine, :] = jnp.where(outer, pltpu.roll(parts[q], LANES - 4, 1), sbuf[mine, :])

    @pl.when((me != first_in) & (me != herald))
    def _():
        pl.semaphore_wait(first_sem, 1)

    @pl.when(me != first_in)
    def _():
        block_copy(lbuf, rbuf, 0)(first_in)

    exchange(block_copy(lbuf, rbuf, 0), early)
    keep(lbuf, rbuf)

    for load in loads[2:]:
        load.wait()
    slots = cells_ref.shape[1]
    live = lax.broadcasted_iota(jnp.int32, (1, slots), 1) < count_ref[0]
    wts = jnp.where(live, weight_ref[...], 0.0)
    wval = wts * value_ref[...]
    dsum = [jnp.zeros((8, LANES), F32) for _ in range(HEIGHT)]
    esum = [jnp.zeros((8, LANES), F32) for _ in range(HEIGHT)]
    cell_of = lax.broadcasted_iota(jnp.int32, (LANES, LANES), 1)
    for k in range(slots // LANES):
        part = slice(k * LANES, (k + 1) * LANES)
        cs = jnp.broadcast_to(cells_ref[:, part], (LANES, LANES)).T
        ws = jnp.broadcast_to(wts[:, part], (LANES, LANES)).T
        vs = jnp.broadcast_to(wval[:, part], (LANES, LANES)).T
        for j in range(HEIGHT):
            hit = cs == cell_of + j * LANES
            dsum[j] += jnp.sum(jnp.where(hit, ws, 0.0).reshape(LANES // 8, 8, LANES), axis=0)
            esum[j] += jnp.sum(jnp.where(hit, vs, 0.0).reshape(LANES // 8, 8, LANES), axis=0)
    dcell = [jnp.sum(x, axis=0, keepdims=True) for x in dsum]
    ecell = [jnp.sum(x, axis=0, keepdims=True) for x in esum]

    settle(rbuf, 0, recv_sem)
    edges = erecv.at[pl.ds(0, early * ring * 2)]
    if early:
        @pl.when(me != first_in)
        def _():
            pltpu.make_async_copy(edges, edges, recv_sem.at[2]).wait()

    got = erecv[...].reshape(G, LANES)
    ahead = lax.rem(column_of - lax.broadcasted_iota(jnp.int32, (G, LANES), 0) // (ring * 2) + columns, columns)
    ahead = jnp.where(me == first_in, columns, ahead)
    outer &= functools.reduce(jnp.logical_or, [ahead == dx for dx in across[:early]], ahead < 0)

    mean = []
    rcell = []
    scaled = []
    for j in range(HEIGHT):
        x = jnp.concatenate(
            [jnp.where(outer, pltpu.roll(got, (LANES - 4 - 8 * (ml * HEIGHT + j)) % LANES, 1),
                       rbuf[pl.ds(ml * HEIGHT + j, G, stride=block), :]) for ml in range(members)],
            axis=0)
        mu = jnp.sum(x, axis=0, keepdims=True) * (1.0 / order)
        p = x - mu
        hi, lo = split(p)
        cols = slice(j * LANES, (j + 1) * LANES)
        pert_hi[:, cols] = hi
        pert_lo[:, cols] = lo
        scaled.append(split(p * dcell[j]))
        mean.append(mu)
        rcell.append(ecell[j] - dcell[j] * mu)
    a_hi = jnp.concatenate([s[0] for s in scaled], axis=1)
    a_lo = jnp.concatenate([s[1] for s in scaled], axis=1)
    nt = (((1,), (1,)), ((), ()))
    eye = (lax.broadcasted_iota(jnp.int32, (order, order), 0)
           == lax.broadcasted_iota(jnp.int32, (order, order), 1))
    gram = lax.dot_general(
        jnp.concatenate([a_hi, a_hi, a_lo], axis=1),
        jnp.concatenate([pert_hi[...], pert_lo[...], pert_hi[...]], axis=1),
        nt, preferred_element_type=F32)
    gram = gram + jnp.where(eye, order - 1.0, 0.0)
    total = jnp.sum(jnp.sum(gram * gram, axis=0, keepdims=True), axis=1, keepdims=True) + 1e-06
    scale = jnp.sqrt(total)
    y = gram / scale
    diag = jnp.where(eye, 1.5, 0.0)
    mid = diag - 0.5 * y
    ms = split(mid)
    y = mul3(split(y), ms)
    zmat = mid
    for step in range(1, NS_ITERS):
        ys, zs = split(y), split(zmat)
        ms = split(diag - 0.5 * mul3(zs, ys))
        if step < NS_ITERS - 1:
            y = mul3(ys, ms)
        zmat = mul3(zs, ms)
    root = zmat / jnp.sqrt(scale)
    dev = mul3(split(root), (pert_hi[...], pert_lo[...]))
    u = jnp.zeros((order, 1), F32)
    for j in range(HEIGHT):
        u = u + jnp.sum(dev[:, j * LANES:(j + 1) * LANES] * rcell[j], axis=1, keepdims=True)
    for j in range(HEIGHT):
        dj = dev[:, j * LANES:(j + 1) * LANES]
        shift = mean[j] + jnp.sum(dj * u, axis=0, keepdims=True)
        res = shift + jnp.sqrt(jnp.full((1, 1), order - 1.0, F32)) * dj
        for ml in range(members):
            tbuf[pl.ds(ml * HEIGHT + j, G, stride=block), :] = res[ml * G:(ml + 1) * G, :]

    exchange(block_copy(tbuf, obuf, 1), all_members=True)
    keep(tbuf, obuf)
    settle(sbuf, 0, send_sem)
    if early:
        some = erecv.at[pl.ds(0, early * ring * 2 - 1)]

        @pl.when(column_of != 0)
        def _():
            pltpu.make_async_copy(some, some, send_sem.at[2]).wait()

        @pl.when(column_of == 0)
        def _():
            pltpu.make_async_copy(edges, edges, send_sem.at[2]).wait()

    settle(obuf, 1, recv_sem)
    settle(obuf, 1, send_sem)


def place_kernel(blocks_ref, out_hbm, tile, sem):
    rows = blocks_ref.shape[0]
    G = lax.axis_size("member")
    ny = G * HEIGHT
    members = rows // ny
    copies = []
    for ml in range(members):
        for j in range(HEIGHT):
            tile[pl.ds(ml * ny + j, G, stride=HEIGHT), :] = blocks_ref[
                pl.ds(ml * HEIGHT + j, G, stride=members * HEIGHT), :]
        span = pl.ds(ml * ny, ny)
        copies.append(pltpu.make_async_copy(tile.at[span, :], out_hbm.at[span, :], sem.at[ml]))
        copies[-1].start()
    for copy in copies:
        copy.wait()


def local(prior_ensemble, wind, obs_value, obs_weight, observed_cell_value, obs_count):
    members, ny, columns = prior_ensemble.shape
    rows = members * ny
    order = members * lax.axis_size("member")
    prior = prior_ensemble.reshape(rows, columns)
    vmem = pl.BlockSpec(memory_space=pltpu.VMEM)
    hbm = pl.BlockSpec(memory_space=pltpu.HBM)
    slots = obs_value.shape[1]
    big = pltpu.VMEM((rows, LANES), F32)
    strip = pltpu.VMEM((8, rows + ny), F32)
    half = pltpu.VMEM((order, HEIGHT * LANES), BF16)
    dma = pltpu.SemaphoreType.DMA
    blocks = pl.pallas_call(
        main_kernel,
        out_shape=pltpu.VMEM((rows, columns), F32),
        in_specs=[hbm] * 6,
        out_specs=vmem,
        scratch_shapes=[
            pltpu.SMEM((1,), jnp.int32), big, pltpu.VMEM((ny, LANES), F32),
            pltpu.VMEM((1, slots), F32), pltpu.VMEM((1, slots), F32),
            pltpu.VMEM((1, slots), jnp.int32)]
        + [pltpu.VMEM((24, rows + ny), F32)] + [strip] * 2 + [big] * 5
        + [pltpu.VMEM((order // members, 1, LANES), F32)] * 2 + [half] * 2
        + [dma((6,)), dma((2,)), dma((2,)), dma((3,)), dma((3,))]
        + [pltpu.SemaphoreType.REGULAR] * 3,
        compiler_params=pltpu.CompilerParams(
            collective_id=0, has_side_effects=True, vmem_limit_bytes=VMEM_BYTES),
        name="forecast_analysis",
    )(obs_count, *(pltpu.with_memory_space_constraint(a, pltpu.HBM) for a in (
        prior, wind, obs_value, obs_weight, observed_cell_value)))
    out = pl.pallas_call(
        place_kernel,
        out_shape=jax.ShapeDtypeStruct((rows, columns), F32),
        in_specs=[vmem],
        out_specs=hbm,
        scratch_shapes=[big, dma((members,))],
        compiler_params=pltpu.CompilerParams(vmem_limit_bytes=4 * 1024 * 1024),
        name="place",
    )(pltpu.with_memory_space_constraint(blocks, pltpu.VMEM))
    return out.reshape(members, ny, columns)


def solution(mesh):
    in_specs = (
        P("member", None, "space"),
        P(None, "space"),
        P(("space", "member"), None),
        P(("space", "member"), None),
        P(("space", "member"), None),
        P(("space", "member")),
    )
    out_specs = P("member", None, "space")
    return jax.shard_map(local, mesh=mesh, in_specs=in_specs, out_specs=out_specs, check_vma=False)
```
